128 devices in a mesh: img: 128 (over x, z, y, core).
Axes of the slice: x: 4, y: 4, z: 4, core: 2. Of those that a mesh axis runs over, the one named last changes fastest.
Arguments:
- queries: bfloat16 [49152, 1024], P('img'), may hold values from -10 to 10
- keys: bfloat16 [49152, 1024], P('img'), may hold values from -10 to 10
- values: bfloat16 [49152, 1024], P('img'), may hold values from -6 to 6
- out_grad: bfloat16 [49152, 1024], P('img'), may hold values from -6 to 6
- image_ids: int32 [49152], P('img'), may hold values from 0 to 127, never falling along the last dimension, each value on 1 to 1152 neighbouring positions
Outputs:
- attended: bfloat16 [49152, 1024], P('img')
- query_grad: bfloat16 [49152, 1024], P('img')
- key_grad: bfloat16 [49152, 1024], P('img')
- value_grad: bfloat16 [49152, 1024], P('img')
The draws below stay inside these ranges and needn't reach their ends.
Inputs may be any that keep to these rules, and one draw needn't show every extreme that they name: `image_ids`: the regions of one image stand in consecutive rows, and ids rise along the rows; an image has 1 to 1152 regions, and some image has exactly 1152.
All inputs are finite; a program needn't handle non-finite values.
Results may differ from the reference program's by a relative error of at most 0.0069.
Values may be sent and summed in bfloat16 or wider, within the bound.
No kernel may reach another device: no remote copies, remote signals or barrier semaphores. Data moves between devices by JAX's collectives and lax.ppermute only.
A program may use at most 192 MiB of HBM per device.

```python
import math
import jax
import jax.numpy as jnp
import numpy as np
from jax import lax

D = 1024
HEADS = 16
ROWS_DEV = 384
REACH = 3
MOST = 1152
TOKENS = 49152
N_IMG = 128


def paired_features(key):
    base = jax.random.fold_in(key, 7)
    first, second = jax.random.split(base, 2)
    shape = (TOKENS, D)
    query_f = jnp.clip(jax.random.normal(first, shape, jnp.float32), -6.0, 6.0)
    key_f = jnp.clip(jax.random.normal(second, shape, jnp.float32), -6.0, 6.0)
    return (query_f, key_f)


def draw_queries(key, part):
    return paired_features(key)[0].astype(jnp.bfloat16)


def draw_keys(key, part):
    return paired_features(key)[1].astype(jnp.bfloat16)


def levels(key, extent, cuts, least, top_value):
    gain = 1.0
    for axis_at, shards_of in cuts:
        steps = jax.random.uniform(jax.random.fold_in(jax.random.fold_in(key, 6), axis_at), (shards_of,), jnp.float32, least / len(cuts), top_value / len(cuts))
        gain = gain * jnp.repeat(jnp.exp(steps), extent[axis_at] // shards_of).reshape((-1,) + (1,) * (len(extent) - 1 - axis_at))
    return gain


def profile(amount, total, limit, lean):
    portions = [(1 << 20) // math.isqrt(rank ** lean) + 1 for rank in range(2, amount + 1)]
    spare, holding = total - limit - (amount - 1), [1] * (amount - 1)
    while spare > 0:
        free = [i for i in range(amount - 1) if holding[i] < limit]
        pool, remaining = sum([portions[i] for i in free]), spare
        for i in free:
            more = min(limit - holding[i], max(1, remaining * portions[i] // pool), spare)
            holding[i] = holding[i] + more
            spare = spare - more
    return np.array([limit] + holding)


def ragged_sizes(own_key, amount, total, limit, lean):
    if amount == 2:
        one = jax.random.randint(own_key, (), max(1, total - limit), min(limit, total - 1) + 1)
        return jnp.stack([one, total - one])
    tallies = jnp.asarray(profile(amount, total, limit, lean), jnp.int32)
    twos = (amount - 1) // 2
    donor, taker = tallies[1:1 + 2 * twos:2], tallies[2:2 + 2 * twos:2]
    room = jnp.minimum(donor - 1, limit - taker)
    shifted = jax.random.randint(jax.random.fold_in(own_key, 1), (twos,), 0, 1 << 20) % (room + 1)
    tallies = tallies.at[1:1 + 2 * twos:2].set(donor - shifted).at[2:2 + 2 * twos:2].set(taker + shifted)
    return tallies[jax.random.permutation(jax.random.fold_in(own_key, 2), amount)]


def bell_draw(own_key, dims, spread, reach, cuts=(), held_as=jnp.bfloat16):
    drawn = spread * jax.random.normal(own_key, dims, jnp.float32)
    if cuts:
        drawn = drawn * levels(own_key, dims, cuts, -0.22, 0.18)
    return jnp.clip(drawn, -reach, reach).astype(held_as)


def setup_inputs(seed: int = 0) -> dict:
    arg_keys = jax.random.split(jax.random.key(seed), 6)
    return {
        "queries": draw_queries(jax.random.fold_in(arg_keys[5], 71), 0),
        "keys": draw_keys(jax.random.fold_in(arg_keys[5], 71), 0),
        "values": bell_draw(arg_keys[2], (TOKENS, D), 1.0, 6.0, ((0, 128),)),
        "out_grad": bell_draw(arg_keys[3], (TOKENS, D), 1.0, 6.0, ((0, 128),)),
        "image_ids": jnp.searchsorted(jnp.cumsum(ragged_sizes(arg_keys[4], N_IMG, TOKENS, MOST, 1)), jnp.arange(TOKENS), side="right").astype(jnp.int32),
    }


def attend_block(query_rows, key_rows, value_rows, grad_rows, query_tags, key_tags):
    row_count = query_rows.shape[0]
    width = key_rows.shape[0]
    head_dim = D // HEADS
    score_scale = 1.0 / math.sqrt(head_dim)
    query_f = query_rows.astype(jnp.float32).reshape(row_count, HEADS, head_dim)
    key_f = key_rows.astype(jnp.float32).reshape(width, HEADS, head_dim)
    value_f = value_rows.astype(jnp.float32).reshape(width, HEADS, head_dim)
    grad_f = grad_rows.astype(jnp.float32).reshape(row_count, HEADS, head_dim)
    same_image = query_tags[:, None] == key_tags[None, :]
    scores = jnp.einsum('rhd,whd->hrw', query_f, key_f) * score_scale
    scores = jnp.where(same_image[None], scores, -1e+30)
    peak = lax.optimization_barrier(jnp.max(scores, axis=-1, keepdims=True))
    weights = jnp.exp(scores - peak)
    probs = weights / lax.optimization_barrier(jnp.sum(weights, axis=-1, keepdims=True))
    probs_b = lax.optimization_barrier(probs.astype(jnp.bfloat16)).astype(jnp.float32)
    attended = jnp.einsum('hrw,whd->rhd', probs_b, value_f).reshape(row_count, D).astype(jnp.bfloat16)
    dprobs = jnp.einsum('rhd,whd->hrw', grad_f, value_f)
    row_delta = lax.optimization_barrier(jnp.sum(probs * dprobs, axis=-1, keepdims=True))
    dscores = probs * (dprobs - row_delta)
    dscores_b = lax.optimization_barrier(dscores.astype(jnp.bfloat16)).astype(jnp.float32)
    query_grad = (jnp.einsum('hrw,whd->rhd', dscores_b, key_f) * score_scale).reshape(row_count, D).astype(jnp.bfloat16)
    key_grad = (jnp.einsum('hrw,rhd->whd', dscores_b, query_f) * score_scale).reshape(width, D)
    value_grad = jnp.einsum('hrw,rhd->whd', probs_b, grad_f).reshape(width, D)
    return (attended, query_grad, key_grad, value_grad)

def reference(queries, keys, values, out_grad, image_ids):
    row_count = ROWS_DEV
    width = (2 * REACH + 1) * row_count
    margin = REACH * row_count
    image_tags = (image_ids + 1).astype(jnp.int32)
    keys_padded = jnp.pad(keys, ((margin, margin), (0, 0)))
    values_padded = jnp.pad(values, ((margin, margin), (0, 0)))
    tags_padded = jnp.pad(image_tags, (margin, margin))
    start_acc = (jnp.zeros((TOKENS + 2 * margin, D), jnp.float32), jnp.zeros((TOKENS + 2 * margin, D), jnp.float32))

    def one_block(carry, block):
        key_acc, value_acc = carry
        start = (block * row_count).astype(jnp.int32)
        query_rows = lax.dynamic_slice_in_dim(queries, start, row_count, 0)
        grad_rows = lax.dynamic_slice_in_dim(out_grad, start, row_count, 0)
        query_tags = lax.dynamic_slice_in_dim(image_tags, start, row_count, 0)
        key_rows = lax.dynamic_slice_in_dim(keys_padded, start, width, 0)
        value_rows = lax.dynamic_slice_in_dim(values_padded, start, width, 0)
        key_tags = lax.dynamic_slice_in_dim(tags_padded, start, width, 0)
        attended, query_grad, key_grad, value_grad = attend_block(query_rows, key_rows, value_rows, grad_rows, query_tags, key_tags)
        key_acc = lax.dynamic_update_slice_in_dim(key_acc, lax.dynamic_slice_in_dim(key_acc, start, width, 0) + key_grad, start, 0)
        value_acc = lax.dynamic_update_slice_in_dim(value_acc, lax.dynamic_slice_in_dim(value_acc, start, width, 0) + value_grad, start, 0)
        return ((key_acc, value_acc), (attended, query_grad))
    (key_acc, value_acc), (attended, query_grad) = lax.scan(one_block, start_acc, jnp.arange(N_IMG, dtype=jnp.int32))
    attended = attended.reshape(TOKENS, D)
    query_grad = query_grad.reshape(TOKENS, D)
    key_grad = key_acc[margin:margin + TOKENS].astype(jnp.bfloat16)
    value_grad = value_acc[margin:margin + TOKENS].astype(jnp.bfloat16)
    return (attended, query_grad, key_grad, value_grad)
```

```python
import math

import jax
import jax.numpy as jnp
from jax import lax
from jax.experimental import pallas as pl
from jax.experimental.pallas import tpu as pltpu
from jax.sharding import PartitionSpec as P

D = 1024
HEADS = 16
HEAD_DIM = 64
ROWS = 384
MOST = 1152
N_IMG = 128
GROUP = 8
GROUPS = N_IMG // GROUP
GROUP_ROWS = GROUP * ROWS
REACH = 3
LANES = 128
EXT_ROWS = GROUP_ROWS + 2 * MOST
K_STEP = 256
PAD_ROWS = EXT_ROWS + K_STEP
TILES = GROUP_ROWS // LANES
TAG_ROWS = 16
MAX_STEPS = 11
SCALE = 1.0 / math.sqrt(HEAD_DIM)
EXP_SCALE = SCALE * math.log2(math.e)
NEG = -1e30


def group_lists():
    return [[g * GROUP + i for i in range(GROUP)] for g in range(GROUPS)]


def shifted(value, steps):
    leading, last = max(0, -steps), min(N_IMG, N_IMG - steps)
    return lax.ppermute(value, "img", [(s, s + steps) for s in range(leading, last)])


def dot_nt(a, b):
    return lax.dot_general(a, b, (((1,), (1,)), ((), ())), preferred_element_type=jnp.float32)


def dot_nn(a, b):
    return lax.dot_general(a, b, (((1,), (0,)), ((), ())), preferred_element_type=jnp.float32)


def fold_rows(x):
    return x.reshape(x.shape[0] // 8, 8, x.shape[1])


def attend_kernel(
    lo_ref, hi_ref, start_ref, end_ref, own_ref, left_ref, right_ref, qg_ref,
    oq_ref, own_kv_ref, left_kv_ref, right_kv_ref,
    kx, vx, kt, vt, dk, dv, sbuf, dbuf, ot, qt,
):
    for j in range(REACH):
        a = j * ROWS
        b = MOST + GROUP_ROWS + j * ROWS
        kx[a : a + ROWS, :] = left_ref[j, 0:ROWS, :]
        vx[a : a + ROWS, :] = left_ref[j, ROWS : 2 * ROWS, :]
        kx[b : b + ROWS, :] = right_ref[j, 0:ROWS, :]
        vx[b : b + ROWS, :] = right_ref[j, ROWS : 2 * ROWS, :]
    for j in range(GROUP):
        a = MOST + j * ROWS
        kx[a : a + ROWS, :] = own_ref[j, 0:ROWS, :]
        vx[a : a + ROWS, :] = own_ref[j, ROWS : 2 * ROWS, :]
    kx[EXT_ROWS:PAD_ROWS, :] = jnp.zeros((PAD_ROWS - EXT_ROWS, LANES), jnp.bfloat16)
    vx[EXT_ROWS:PAD_ROWS, :] = jnp.zeros((PAD_ROWS - EXT_ROWS, LANES), jnp.bfloat16)
    dk[...] = jnp.zeros_like(dk)
    dv[...] = jnp.zeros_like(dv)

    def transpose_chunk(c, _):
        at = pl.multiple_of(c * LANES, LANES)
        kt[:, pl.ds(at, LANES)] = kx[pl.ds(at, LANES), :].T
        vt[:, pl.ds(at, LANES)] = vx[pl.ds(at, LANES), :].T
        return 0

    lax.fori_loop(0, PAD_ROWS // LANES, transpose_chunk, 0)

    lane = lax.broadcasted_iota(jnp.int32, (LANES, LANES), 1)
    first_head = lane < HEAD_DIM
    row_index = lax.broadcasted_iota(jnp.int32, (K_STEP, 2 * LANES), 0)

    def q_tile(t, _):
        dev = t // REACH
        off = pl.multiple_of((t % REACH) * LANES, LANES)
        q = qg_ref[dev, pl.ds(off, LANES), :]
        g = qg_ref[dev, pl.ds(off + ROWS, LANES), :]
        zero = jnp.zeros_like(q)
        q2 = jnp.concatenate([jnp.where(first_head, q, zero), jnp.where(first_head, zero, q)], 0)
        g2 = jnp.concatenate([jnp.where(first_head, g, zero), jnp.where(first_head, zero, g)], 0)
        begin = start_ref[pl.ds(t, 1), :]
        stop = end_ref[pl.ds(t, 1), :]
        begin = jnp.concatenate([begin, begin], 1)
        stop = jnp.concatenate([stop, stop], 1)
        k0 = (lo_ref[t] // LANES) * LANES
        steps = (hi_ref[t] - k0 + K_STEP - 1) // K_STEP

        def scores(i, top):
            at = pl.multiple_of(k0 + i * K_STEP, LANES)
            s = dot_nt(kx[pl.ds(at, K_STEP), :], q2)
            index = row_index + at
            s = jnp.where((index >= begin) & (index < stop), s, NEG)
            sbuf[pl.ds(pl.multiple_of(i * K_STEP, K_STEP), K_STEP), :] = s
            return jnp.maximum(top, jnp.max(fold_rows(s), axis=0))

        top = lax.fori_loop(0, steps, scores, jnp.full((8, 2 * LANES), NEG, jnp.float32))
        top = jnp.max(top, axis=0, keepdims=True)

        def weigh(i, carry):
            total, delta = carry
            at = pl.multiple_of(k0 + i * K_STEP, LANES)
            here = pl.ds(pl.multiple_of(i * K_STEP, K_STEP), K_STEP)
            e = jnp.exp2((sbuf[here, :] - top) * EXP_SCALE)
            d = dot_nt(vx[pl.ds(at, K_STEP), :], g2)
            sbuf[here, :] = e
            dbuf[here, :] = d
            total = total + jnp.sum(fold_rows(e), axis=0)
            delta = delta + jnp.sum(fold_rows(e * d), axis=0)
            return total, delta

        zeros8 = jnp.zeros((8, 2 * LANES), jnp.float32)
        total, delta = lax.fori_loop(0, steps, weigh, (zeros8, zeros8))
        inverse = 1.0 / jnp.sum(total, axis=0, keepdims=True)
        delta = jnp.sum(delta, axis=0, keepdims=True) * inverse
        ot[...] = jnp.zeros_like(ot)
        qt[...] = jnp.zeros_like(qt)

        def spread(i, _):
            at = pl.multiple_of(k0 + i * K_STEP, LANES)
            here = pl.ds(pl.multiple_of(i * K_STEP, K_STEP), K_STEP)
            rows = pl.ds(at, K_STEP)
            p = sbuf[here, :] * inverse
            ds = (p * (dbuf[here, :] - delta)).astype(jnp.bfloat16)
            p = p.astype(jnp.bfloat16)
            dv[rows, :] += dot_nn(p, g2)
            dk[rows, :] += dot_nn(ds, q2)
            ot[...] += dot_nn(vt[:, rows], p)
            qt[...] += dot_nn(kt[:, rows], ds)
            return 0

        lax.fori_loop(0, steps, spread, 0)
        o = jnp.concatenate([ot[0:HEAD_DIM, 0:LANES], ot[HEAD_DIM:LANES, LANES : 2 * LANES]], 0)
        dq = jnp.concatenate([qt[0:HEAD_DIM, 0:LANES], qt[HEAD_DIM:LANES, LANES : 2 * LANES]], 0)
        oq_ref[dev, pl.ds(off, LANES), :] = o.T.astype(jnp.bfloat16)
        oq_ref[dev, pl.ds(off + ROWS, LANES), :] = (dq.T * SCALE).astype(jnp.bfloat16)
        return 0

    lax.fori_loop(0, TILES, q_tile, 0)
    left_kv_ref[0] = (dk[0:MOST, :] * SCALE).astype(jnp.bfloat16)
    left_kv_ref[1] = dv[0:MOST, :].astype(jnp.bfloat16)
    right_kv_ref[0] = (dk[MOST + GROUP_ROWS : EXT_ROWS, :] * SCALE).astype(jnp.bfloat16)
    right_kv_ref[1] = dv[MOST + GROUP_ROWS : EXT_ROWS, :].astype(jnp.bfloat16)
    own_kv_ref[0] = dk[MOST : MOST + GROUP_ROWS, :] * SCALE
    own_kv_ref[1] = dv[MOST : MOST + GROUP_ROWS, :]


def attend(lo, hi, start, end, own, left, right, qg):
    smem = pl.BlockSpec(memory_space=pltpu.SMEM)
    vmem = pl.BlockSpec(memory_space=pltpu.VMEM)
    bf16, f32 = jnp.bfloat16, jnp.float32
    return pl.pallas_call(
        attend_kernel,
        out_shape=(
            jax.ShapeDtypeStruct((GROUP, 2 * ROWS, LANES), bf16),
            jax.ShapeDtypeStruct((2, GROUP_ROWS, LANES), f32),
            jax.ShapeDtypeStruct((2, MOST, LANES), bf16),
            jax.ShapeDtypeStruct((2, MOST, LANES), bf16),
        ),
        in_specs=[smem, smem] + [vmem] * 6,
        out_specs=(vmem,) * 4,
        scratch_shapes=[
            pltpu.VMEM((PAD_ROWS, LANES), bf16),
            pltpu.VMEM((PAD_ROWS, LANES), bf16),
            pltpu.VMEM((LANES, PAD_ROWS), bf16),
            pltpu.VMEM((LANES, PAD_ROWS), bf16),
            pltpu.VMEM((PAD_ROWS, LANES), f32),
            pltpu.VMEM((PAD_ROWS, LANES), f32),
            pltpu.VMEM((MAX_STEPS * K_STEP, 2 * LANES), f32),
            pltpu.VMEM((MAX_STEPS * K_STEP, 2 * LANES), f32),
            pltpu.VMEM((LANES, 2 * LANES), f32),
            pltpu.VMEM((LANES, 2 * LANES), f32),
        ],
        compiler_params=pltpu.CompilerParams(vmem_limit_bytes=48 * 1024 * 1024),
        cost_estimate=pl.CostEstimate(
            flops=20_000_000_000, bytes_accessed=12_000_000, transcendentals=6_000_000
        ),
        name="attend",
    )(lo, hi, start, end, own, left, right, qg)


def split_heads(x):
    return x.reshape(ROWS, GROUP, LANES).transpose(1, 0, 2)


def exchange(x):
    return lax.all_to_all(x, "img", 0, 0, axis_index_groups=group_lists())


def merge_heads(x):
    return x.transpose(1, 0, 2).reshape(ROWS, D)


def shards(queries, keys, values, out_grad, image_ids):
    tags = (image_ids + 1).astype(jnp.bfloat16).reshape(ROWS // LANES, LANES)
    tags = jnp.pad(tags, ((0, TAG_ROWS - ROWS // LANES), (0, 0)))
    tags = jnp.broadcast_to(tags[None], (GROUP, TAG_ROWS, LANES))
    own = exchange(jnp.concatenate([split_heads(keys), split_heads(values), tags], 1))
    left = shifted(own[GROUP - REACH :], GROUP)
    right = shifted(own[:REACH], -GROUP)
    qg = exchange(jnp.concatenate([split_heads(queries), split_heads(out_grad)], 1))

    def tags_of(x):
        return x[:, 2 * ROWS : 2 * ROWS + ROWS // LANES, :].astype(jnp.int32).reshape(-1)

    own_tags = tags_of(own)
    right_tags = tags_of(right)
    is_last = lax.axis_index("img") >= N_IMG - GROUP
    right_tags = jnp.where(is_last, N_IMG + 1, right_tags)
    ext_tags = jnp.concatenate([tags_of(left), own_tags, right_tags])
    every = jnp.arange(N_IMG + 1, dtype=jnp.int32)
    below = jnp.sum((ext_tags[None, :] < every[:, None]).astype(jnp.int32), 1)
    upto = jnp.sum((ext_tags[None, :] <= every[:, None]).astype(jnp.int32), 1)
    pick = own_tags[:, None] == every[None, :]
    start = jnp.sum(jnp.where(pick, below[None, :], 0), 1).reshape(TILES, LANES)
    end = jnp.sum(jnp.where(pick, upto[None, :], 0), 1).reshape(TILES, LANES)
    oq, own_kv, left_kv, right_kv = attend(
        start[:, 0], end[:, LANES - 1], start, end, own, left, right, qg
    )
    from_next = shifted(left_kv, -GROUP)
    from_prev = shifted(right_kv, GROUP)
    oq = exchange(oq)
    kv = own_kv.at[:, GROUP_ROWS - MOST :].add(from_next.astype(jnp.float32))
    kv = kv.at[:, :MOST].add(from_prev.astype(jnp.float32))
    kv = kv.astype(jnp.bfloat16).reshape(2, GROUP, ROWS, LANES).transpose(1, 0, 2, 3)
    kv = exchange(kv.reshape(GROUP, 2 * ROWS, LANES))
    return (
        merge_heads(oq[:, :ROWS]),
        merge_heads(oq[:, ROWS:]),
        merge_heads(kv[:, :ROWS]),
        merge_heads(kv[:, ROWS:]),
    )


def solution(mesh):
    in_specs = (P("img", None), P("img", None), P("img", None), P("img", None), P("img"))
    out_specs = (P("img", None), P("img", None), P("img", None), P("img", None))
    return jax.shard_map(shards, mesh=mesh, in_specs=in_specs, out_specs=out_specs, check_vma=False)
```

```python
import math

import jax
import jax.numpy as jnp
from jax import lax
from jax.experimental import pallas as pl
from jax.experimental.pallas import tpu as pltpu
from jax.sharding import PartitionSpec as P

D = 1024
HEAD_DIM = 64
ROWS = 384
MOST = 1152
N_IMG = 128
GROUP = 8
GROUPS = N_IMG // GROUP
GROUP_ROWS = GROUP * ROWS
REACH = 3
LANES = 128
EXT_ROWS = GROUP_ROWS + 2 * MOST
K_STEP = 256
PAD_ROWS = EXT_ROWS + K_STEP
TILES = GROUP_ROWS // LANES
TAG_ROWS = 16
MAX_STEPS = 11
UNROLLED = 8
PAIR = 2
SCALE = 1.0 / math.sqrt(HEAD_DIM)
EXP_SCALE = SCALE * math.log2(math.e)
NEG = -1e30


def group_lists():
    return [[g * GROUP + i for i in range(GROUP)] for g in range(GROUPS)]


def shifted(value, steps):
    leading, last = max(0, -steps), min(N_IMG, N_IMG - steps)
    return lax.ppermute(value, "img", [(s, s + steps) for s in range(leading, last)])


def dot_nt(a, b):
    return lax.dot_general(a, b, (((1,), (1,)), ((), ())), preferred_element_type=jnp.float32)


def dot_nn(a, b):
    return lax.dot_general(a, b, (((1,), (0,)), ((), ())), preferred_element_type=jnp.float32)


def fold_rows(x):
    return x.reshape(x.shape[0] // 8, 8, x.shape[1])


def attend_kernel(
    lo_ref, hi_ref, start_ref, end_ref, own_ref, left_ref, right_ref, qg_ref,
    oq_ref, own_kv_ref, left_kv_ref, right_kv_ref,
    kx, vx, kt, vt, dk, dv, sbuf, dbuf, ot, qt,
):
    for j in range(REACH):
        a = j * ROWS
        b = MOST + GROUP_ROWS + j * ROWS
        kx[a : a + ROWS, :] = left_ref[j, 0:ROWS, :]
        vx[a : a + ROWS, :] = left_ref[j, ROWS : 2 * ROWS, :]
        kx[b : b + ROWS, :] = right_ref[j, 0:ROWS, :]
        vx[b : b + ROWS, :] = right_ref[j, ROWS : 2 * ROWS, :]
    for j in range(GROUP):
        a = MOST + j * ROWS
        kx[a : a + ROWS, :] = own_ref[j, 0:ROWS, :]
        vx[a : a + ROWS, :] = own_ref[j, ROWS : 2 * ROWS, :]
    kx[EXT_ROWS:PAD_ROWS, :] = jnp.zeros((PAD_ROWS - EXT_ROWS, LANES), jnp.bfloat16)
    vx[EXT_ROWS:PAD_ROWS, :] = jnp.zeros((PAD_ROWS - EXT_ROWS, LANES), jnp.bfloat16)
    dk[...] = jnp.zeros_like(dk)
    dv[...] = jnp.zeros_like(dv)

    def transpose_chunk(c, _):
        at = pl.multiple_of(c * K_STEP, K_STEP)
        kt[:, pl.ds(at, K_STEP)] = kx[pl.ds(at, K_STEP), :].T
        vt[:, pl.ds(at, K_STEP)] = vx[pl.ds(at, K_STEP), :].T
        return 0

    lax.fori_loop(0, PAD_ROWS // K_STEP, transpose_chunk, 0)

    lane = lax.broadcasted_iota(jnp.int32, (LANES, LANES), 1)
    first_head = lane < HEAD_DIM
    row_index = lax.broadcasted_iota(jnp.int32, (K_STEP, LANES), 0)

    def both_heads(x):
        zero = jnp.zeros_like(x)
        return jnp.concatenate([jnp.where(first_head, x, zero), jnp.where(first_head, zero, x)], 0)

    def step_count(t):
        return (hi_ref[t] - (lo_ref[t] // LANES) * LANES + K_STEP - 1) // K_STEP

    def q_tiles(u, _):
        tiles = [u * PAIR + j for j in range(PAIR)]
        steps = step_count(tiles[0])
        for t in tiles[1:]:
            steps = jnp.maximum(steps, step_count(t))
        subs = []
        for j, t in enumerate(tiles):
            dev = t // REACH
            off = pl.multiple_of((t % REACH) * LANES, LANES)
            k0 = jnp.minimum((lo_ref[t] // LANES) * LANES, PAD_ROWS - steps * K_STEP)
            subs.append((j, t, dev, off, k0))

        def tile_part(sub, run):
            j, t, dev, off, k0 = sub
            q2 = both_heads(qg_ref[dev, pl.ds(off, LANES), :])
            g2 = both_heads(qg_ref[dev, pl.ds(off + ROWS, LANES), :])
            begin = start_ref[pl.ds(t, 1), :]
            stop = end_ref[pl.ds(t, 1), :]

            def rows_at(i):
                return pl.ds(pl.multiple_of(k0 + i * K_STEP, LANES), K_STEP)

            def here_at(i):
                return pl.ds(i * K_STEP if isinstance(i, int) else pl.multiple_of(i * K_STEP, K_STEP), K_STEP)

            def scores(i, top):
                s = dot_nt(kx[rows_at(i), :], q2)
                index = row_index + (k0 + i * K_STEP)
                keep = (index >= begin) & (index < stop)
                s = jnp.where(jnp.concatenate([keep, keep], 1), s, NEG)
                sbuf[j, here_at(i), :] = s
                dbuf[j, here_at(i), :] = dot_nt(vx[rows_at(i), :], g2)
                return jnp.maximum(top, jnp.max(fold_rows(s), axis=0))

            def weigh(i, carry):
                top, total, delta = carry
                e = jnp.exp2((sbuf[j, here_at(i), :] - top) * EXP_SCALE)
                sbuf[j, here_at(i), :] = e
                total = total + jnp.sum(fold_rows(e), axis=0)
                delta = delta + jnp.sum(fold_rows(e * dbuf[j, here_at(i), :]), axis=0)
                return top, total, delta

            def spread(i, carry):
                inverse, delta = carry
                rows = rows_at(i)
                p = sbuf[j, here_at(i), :] * inverse
                ds = (p * (dbuf[j, here_at(i), :] - delta)).astype(jnp.bfloat16)
                p = p.astype(jnp.bfloat16)
                dv[rows, :] += dot_nn(p, g2)
                dk[rows, :] += dot_nn(ds, q2)
                o = dot_nn(vt[:, rows], p)
                dq = dot_nn(kt[:, rows], ds)
                parts = ((o, ot), (dq, qt))
                for value, ref in parts:
                    top_part = value[0:HEAD_DIM, 0:LANES]
                    low_part = value[HEAD_DIM:LANES, LANES : 2 * LANES]
                    if isinstance(i, int) and i == 0:
                        ref[j, 0:HEAD_DIM, :] = top_part
                        ref[j, HEAD_DIM:LANES, :] = low_part
                    else:
                        ref[j, 0:HEAD_DIM, :] += top_part
                        ref[j, HEAD_DIM:LANES, :] += low_part
                return carry

            def first():
                top = run(scores, jnp.full((8, 2 * LANES), NEG, jnp.float32))
                return jnp.max(top, axis=0, keepdims=True)

            def second(top):
                zeros8 = jnp.zeros((8, 2 * LANES), jnp.float32)
                _, total, delta = run(weigh, (top, zeros8, zeros8))
                inverse = 1.0 / jnp.sum(total, axis=0, keepdims=True)
                return inverse, jnp.sum(delta, axis=0, keepdims=True) * inverse

            def third(carry):
                run(spread, carry)
                oq_ref[dev, pl.ds(off, LANES), :] = ot[j].T.astype(jnp.bfloat16)
                oq_ref[dev, pl.ds(off + ROWS, LANES), :] = (qt[j].T * SCALE).astype(jnp.bfloat16)

            return first, second, third

        def whole(run):
            parts = [tile_part(sub, run) for sub in subs]
            tops = [p[0]() for p in parts]
            stats = [p[1](top) for p, top in zip(parts, tops)]
            for p, stat in zip(parts, stats):
                p[2](stat)

        def unrolled(count):
            def run(body, carry):
                for i in range(count):
                    carry = body(i, carry)
                return carry

            return lambda: whole(run)

        def looped():
            ot[...] = jnp.zeros_like(ot)
            qt[...] = jnp.zeros_like(qt)
            whole(lambda body, carry: lax.fori_loop(0, steps, body, carry))

        lax.switch(
            jnp.minimum(steps - 1, UNROLLED), [unrolled(c + 1) for c in range(UNROLLED)] + [looped]
        )
        return 0

    lax.fori_loop(0, TILES // PAIR, q_tiles, 0)
    left_kv_ref[0] = (dk[0:MOST, :] * SCALE).astype(jnp.bfloat16)
    left_kv_ref[1] = dv[0:MOST, :].astype(jnp.bfloat16)
    right_kv_ref[0] = (dk[MOST + GROUP_ROWS : EXT_ROWS, :] * SCALE).astype(jnp.bfloat16)
    right_kv_ref[1] = dv[MOST + GROUP_ROWS : EXT_ROWS, :].astype(jnp.bfloat16)
    own_kv_ref[0] = dk[MOST : MOST + GROUP_ROWS, :] * SCALE
    own_kv_ref[1] = dv[MOST : MOST + GROUP_ROWS, :]


def attend(lo, hi, start, end, own, left, right, qg):
    smem = pl.BlockSpec(memory_space=pltpu.SMEM)
    vmem = pl.BlockSpec(memory_space=pltpu.VMEM)
    bf16, f32 = jnp.bfloat16, jnp.float32
    return pl.pallas_call(
        attend_kernel,
        out_shape=(
            jax.ShapeDtypeStruct((GROUP, 2 * ROWS, LANES), bf16),
            jax.ShapeDtypeStruct((2, GROUP_ROWS, LANES), f32),
            jax.ShapeDtypeStruct((2, MOST, LANES), bf16),
            jax.ShapeDtypeStruct((2, MOST, LANES), bf16),
        ),
        in_specs=[smem, smem] + [vmem] * 6,
        out_specs=(vmem,) * 4,
        scratch_shapes=[
            pltpu.VMEM((PAD_ROWS, LANES), bf16),
            pltpu.VMEM((PAD_ROWS, LANES), bf16),
            pltpu.VMEM((LANES, PAD_ROWS), bf16),
            pltpu.VMEM((LANES, PAD_ROWS), bf16),
            pltpu.VMEM((PAD_ROWS, LANES), f32),
            pltpu.VMEM((PAD_ROWS, LANES), f32),
            pltpu.VMEM((PAIR, MAX_STEPS * K_STEP, 2 * LANES), f32),
            pltpu.VMEM((PAIR, MAX_STEPS * K_STEP, 2 * LANES), f32),
            pltpu.VMEM((PAIR, LANES, LANES), f32),
            pltpu.VMEM((PAIR, LANES, LANES), f32),
        ],
        compiler_params=pltpu.CompilerParams(vmem_limit_bytes=48 * 1024 * 1024),
        cost_estimate=pl.CostEstimate(
            flops=20_000_000_000, bytes_accessed=12_000_000, transcendentals=6_000_000
        ),
        name="attend",
    )(lo, hi, start, end, own, left, right, qg)


def pack_kernel(*refs):
    for j in range(GROUP):
        at = 0
        for ref in refs[:-1]:
            rows = ref.shape[0]
            cols = slice(j * LANES, (j + 1) * LANES) if ref.shape[1] == D else slice(None)
            refs[-1][j, at : at + rows, :] = ref[:, cols]
            at += rows


def pack(*sources):
    rows = sum(x.shape[0] for x in sources)
    return pl.pallas_call(
        pack_kernel,
        out_shape=jax.ShapeDtypeStruct((GROUP, rows, LANES), jnp.bfloat16),
        cost_estimate=pl.CostEstimate(flops=0, bytes_accessed=3_200_000, transcendentals=0),
        name="pack",
    )(*sources)


def unpack_kernel(in_ref, x_ref, y_ref):
    for j in range(GROUP):
        cols = slice(j * LANES, (j + 1) * LANES)
        x_ref[:, cols] = in_ref[j, 0:ROWS, :]
        y_ref[:, cols] = in_ref[j, ROWS : 2 * ROWS, :]


def unpack(x):
    flat = jax.ShapeDtypeStruct((ROWS, D), jnp.bfloat16)
    return pl.pallas_call(
        unpack_kernel,
        out_shape=(flat, flat),
        cost_estimate=pl.CostEstimate(flops=0, bytes_accessed=3_200_000, transcendentals=0),
        name="unpack",
    )(x)


def total_kernel(own_ref, prev_ref, next_ref, out_ref):
    for n in range(2):
        for j in range(GROUP):
            x = own_ref[n, j * ROWS : (j + 1) * ROWS, :]
            if j < REACH:
                x = x + prev_ref[n, j * ROWS : (j + 1) * ROWS, :].astype(jnp.float32)
            if j >= GROUP - REACH:
                at = (j - GROUP + REACH) * ROWS
                x = x + next_ref[n, at : at + ROWS, :].astype(jnp.float32)
            out_ref[j, n * ROWS : (n + 1) * ROWS, :] = x.astype(jnp.bfloat16)


def total(own, from_prev, from_next):
    return pl.pallas_call(
        total_kernel,
        out_shape=jax.ShapeDtypeStruct((GROUP, 2 * ROWS, LANES), jnp.bfloat16),
        cost_estimate=pl.CostEstimate(flops=0, bytes_accessed=6_000_000, transcendentals=0),
        name="total",
    )(own, from_prev, from_next)


def exchange(x):
    return lax.all_to_all(x, "img", 0, 0, axis_index_groups=group_lists())


def bounds(own, left, right):
    def tags_of(x):
        return x[:, 2 * ROWS : 2 * ROWS + ROWS // LANES, :].astype(jnp.int32).reshape(-1)

    own_tags = tags_of(own)
    is_last = lax.axis_index("img") >= N_IMG - GROUP
    right_tags = jnp.where(is_last, N_IMG + 1, tags_of(right))
    ext_tags = jnp.concatenate([tags_of(left), own_tags, right_tags])
    every = jnp.arange(N_IMG + 1, dtype=jnp.int32)
    below = jnp.sum((ext_tags[None, :] < every[:, None]).astype(jnp.int32), 1)
    upto = jnp.sum((ext_tags[None, :] <= every[:, None]).astype(jnp.int32), 1)
    pick = own_tags[:, None] == every[None, :]
    start = jnp.sum(jnp.where(pick, below[None, :], 0), 1).reshape(TILES, LANES)
    end = jnp.sum(jnp.where(pick, upto[None, :], 0), 1).reshape(TILES, LANES)
    return start[:, 0], end[:, LANES - 1], start, end


def shards(queries, keys, values, out_grad, image_ids):
    tags = (image_ids + 1).astype(jnp.bfloat16).reshape(ROWS // LANES, LANES)
    tags = jnp.pad(tags, ((0, TAG_ROWS - ROWS // LANES), (0, 0)))
    kv, qg = lax.optimization_barrier((pack(keys, values, tags), pack(queries, out_grad)))
    own = exchange(kv)
    qg = exchange(qg)
    left = shifted(own[GROUP - REACH :], GROUP)
    right = shifted(own[:REACH], -GROUP)
    table = bounds(own, left, right)
    oq, own_kv, left_kv, right_kv = attend(*table, own, left, right, qg)
    oq = exchange(oq)
    from_next = shifted(left_kv, -GROUP)
    from_prev = shifted(right_kv, GROUP)
    attended, query_grad = unpack(oq)
    kv = exchange(total(own_kv, from_prev, from_next))
    key_grad, value_grad = unpack(kv)
    return attended, query_grad, key_grad, value_grad


def solution(mesh):
    in_specs = (P("img", None), P("img", None), P("img", None), P("img", None), P("img"))
    out_specs = (P("img", None), P("img", None), P("img", None), P("img", None))
    return jax.shard_map(shards, mesh=mesh, in_specs=in_specs, out_specs=out_specs, check_vma=False)
```

```python
import math

import jax
import jax.numpy as jnp
from jax import lax
from jax.experimental import pallas as pl
from jax.experimental.pallas import tpu as pltpu
from jax.sharding import PartitionSpec as P

D = 1024
HEAD_DIM = 64
ROWS = 384
MOST = 1152
N_IMG = 128
GROUP = 8
GROUPS = N_IMG // GROUP
GROUP_ROWS = GROUP * ROWS
REACH = 3
LANES = 128
EXT_ROWS = GROUP_ROWS + 2 * MOST
K_STEP = 256
PAD_ROWS = EXT_ROWS + K_STEP
TILES = GROUP_ROWS // LANES
TAG_ROWS = 16
Q_AT = 2 * ROWS + TAG_ROWS
MAX_STEPS = 11
UNROLLED = 8
PAIR = 2
SCALE = 1.0 / math.sqrt(HEAD_DIM)
EXP_SCALE = SCALE * math.log2(math.e)
NEG = -1e30


def group_lists():
    return [[g * GROUP + i for i in range(GROUP)] for g in range(GROUPS)]


def shifted(value, steps):
    leading, last = max(0, -steps), min(N_IMG, N_IMG - steps)
    return lax.ppermute(value, "img", [(s, s + steps) for s in range(leading, last)])


def dot_nt(a, b):
    return lax.dot_general(a, b, (((1,), (1,)), ((), ())), preferred_element_type=jnp.float32)


def dot_nn(a, b):
    return lax.dot_general(a, b, (((1,), (0,)), ((), ())), preferred_element_type=jnp.float32)


def fold_rows(x):
    return x.reshape(x.shape[0] // 8, 8, x.shape[1])


def attend_kernel(
    lo_ref, hi_ref, start_ref, end_ref, own_ref, left_ref, right_ref, g_ref,
    oq_ref, own_kv_ref, left_kv_ref, right_kv_ref,
    kx, vx, kt, vt, dk, dv, sbuf, dbuf, ot, qt,
):
    for j in range(REACH):
        a = j * ROWS
        b = MOST + GROUP_ROWS + j * ROWS
        kx[a : a + ROWS, :] = left_ref[j, 0:ROWS, :]
        vx[a : a + ROWS, :] = left_ref[j, ROWS : 2 * ROWS, :]
        kx[b : b + ROWS, :] = right_ref[j, 0:ROWS, :]
        vx[b : b + ROWS, :] = right_ref[j, ROWS : 2 * ROWS, :]
    for j in range(GROUP):
        a = MOST + j * ROWS
        kx[a : a + ROWS, :] = own_ref[j, 0:ROWS, :]
        vx[a : a + ROWS, :] = own_ref[j, ROWS : 2 * ROWS, :]
    kx[EXT_ROWS:PAD_ROWS, :] = jnp.zeros((PAD_ROWS - EXT_ROWS, LANES), jnp.bfloat16)
    vx[EXT_ROWS:PAD_ROWS, :] = jnp.zeros((PAD_ROWS - EXT_ROWS, LANES), jnp.bfloat16)
    dk[...] = jnp.zeros_like(dk)
    dv[...] = jnp.zeros_like(dv)

    def transpose_chunk(c, _):
        at = pl.multiple_of(c * K_STEP, K_STEP)
        kt[:, pl.ds(at, K_STEP)] = kx[pl.ds(at, K_STEP), :].T
        vt[:, pl.ds(at, K_STEP)] = vx[pl.ds(at, K_STEP), :].T
        return 0

    first_chunk = lo_ref[0] // K_STEP
    last_chunk = jnp.minimum(hi_ref[TILES - 1] // K_STEP + 2, PAD_ROWS // K_STEP)
    kt[...] = jnp.zeros_like(kt)
    vt[...] = jnp.zeros_like(vt)
    lax.fori_loop(first_chunk, last_chunk, transpose_chunk, 0)

    lane = lax.broadcasted_iota(jnp.int32, (LANES, LANES), 1)
    first_head = lane < HEAD_DIM
    row_index = lax.broadcasted_iota(jnp.int32, (K_STEP, LANES), 0)

    def both_heads(x):
        zero = jnp.zeros_like(x)
        return jnp.concatenate([jnp.where(first_head, x, zero), jnp.where(first_head, zero, x)], 0)

    def step_count(t):
        return (hi_ref[t] - (lo_ref[t] // LANES) * LANES + K_STEP - 1) // K_STEP

    def q_tiles(u, _):
        tiles = [u * PAIR + j for j in range(PAIR)]
        steps = step_count(tiles[0])
        for t in tiles[1:]:
            steps = jnp.maximum(steps, step_count(t))
        subs = []
        for j, t in enumerate(tiles):
            dev = t // REACH
            off = pl.multiple_of((t % REACH) * LANES, LANES)
            k0 = jnp.minimum((lo_ref[t] // LANES) * LANES, PAD_ROWS - steps * K_STEP)
            subs.append((j, t, dev, off, k0))

        def tile_part(sub, run):
            j, t, dev, off, k0 = sub
            q2 = both_heads(own_ref[dev, pl.ds(pl.multiple_of(off + Q_AT, TAG_ROWS), LANES), :])
            g2 = both_heads(g_ref[dev, pl.ds(off, LANES), :])
            begin = start_ref[pl.ds(t, 1), :]
            stop = end_ref[pl.ds(t, 1), :]

            def rows_at(i):
                return pl.ds(pl.multiple_of(k0 + i * K_STEP, LANES), K_STEP)

            def here_at(i):
                return pl.ds(i * K_STEP if isinstance(i, int) else pl.multiple_of(i * K_STEP, K_STEP), K_STEP)

            def scores(i, top):
                s = dot_nt(kx[rows_at(i), :], q2)
                index = row_index + (k0 + i * K_STEP)
                keep = (index >= begin) & (index < stop)
                s = jnp.where(jnp.concatenate([keep, keep], 1), s, NEG)
                sbuf[j, here_at(i), :] = s
                dbuf[j, here_at(i), :] = dot_nt(vx[rows_at(i), :], g2)
                return jnp.maximum(top, jnp.max(fold_rows(s), axis=0))

            def weigh(i, carry):
                top, total, delta = carry
                e = jnp.exp2((sbuf[j, here_at(i), :] - top) * EXP_SCALE)
                sbuf[j, here_at(i), :] = e
                total = total + jnp.sum(fold_rows(e), axis=0)
                delta = delta + jnp.sum(fold_rows(e * dbuf[j, here_at(i), :]), axis=0)
                return top, total, delta

            def spread(i, carry):
                inverse, delta = carry
                rows = rows_at(i)
                p = sbuf[j, here_at(i), :] * inverse
                ds = (p * (dbuf[j, here_at(i), :] - delta)).astype(jnp.bfloat16)
                p = p.astype(jnp.bfloat16)
                dv[rows, :] += dot_nn(p, g2)
                dk[rows, :] += dot_nn(ds, q2)
                o = dot_nn(vt[:, rows], p)
                dq = dot_nn(kt[:, rows], ds)
                parts = ((o, ot), (dq, qt))
                for value, ref in parts:
                    top_part = value[0:HEAD_DIM, 0:LANES]
                    low_part = value[HEAD_DIM:LANES, LANES : 2 * LANES]
                    if isinstance(i, int) and i == 0:
                        ref[j, 0:HEAD_DIM, :] = top_part
                        ref[j, HEAD_DIM:LANES, :] = low_part
                    else:
                        ref[j, 0:HEAD_DIM, :] += top_part
                        ref[j, HEAD_DIM:LANES, :] += low_part
                return carry

            def first():
                top = run(scores, jnp.full((8, 2 * LANES), NEG, jnp.float32))
                return jnp.max(top, axis=0, keepdims=True)

            def second(top):
                zeros8 = jnp.zeros((8, 2 * LANES), jnp.float32)
                _, total, delta = run(weigh, (top, zeros8, zeros8))
                inverse = 1.0 / jnp.sum(total, axis=0, keepdims=True)
                return inverse, jnp.sum(delta, axis=0, keepdims=True) * inverse

            def third(carry):
                run(spread, carry)
                oq_ref[dev, pl.ds(off, LANES), :] = ot[j].T.astype(jnp.bfloat16)
                oq_ref[dev, pl.ds(off + ROWS, LANES), :] = (qt[j].T * SCALE).astype(jnp.bfloat16)

            return first, second, third

        def whole(run):
            parts = [tile_part(sub, run) for sub in subs]
            tops = [p[0]() for p in parts]
            stats = [p[1](top) for p, top in zip(parts, tops)]
            for p, stat in zip(parts, stats):
                p[2](stat)

        def unrolled(count):
            def run(body, carry):
                for i in range(count):
                    carry = body(i, carry)
                return carry

            return lambda: whole(run)

        def looped():
            ot[...] = jnp.zeros_like(ot)
            qt[...] = jnp.zeros_like(qt)
            whole(lambda body, carry: lax.fori_loop(0, steps, body, carry))

        lax.switch(
            jnp.minimum(steps - 1, UNROLLED), [unrolled(c + 1) for c in range(UNROLLED)] + [looped]
        )
        return 0

    lax.fori_loop(0, TILES // PAIR, q_tiles, 0)
    left_kv_ref[0] = (dk[0:MOST, :] * SCALE).astype(jnp.bfloat16)
    left_kv_ref[1] = dv[0:MOST, :].astype(jnp.bfloat16)
    right_kv_ref[0] = (dk[MOST + GROUP_ROWS : EXT_ROWS, :] * SCALE).astype(jnp.bfloat16)
    right_kv_ref[1] = dv[MOST + GROUP_ROWS : EXT_ROWS, :].astype(jnp.bfloat16)
    own_kv_ref[0] = (dk[MOST : MOST + GROUP_ROWS, :] * SCALE).astype(jnp.bfloat16)
    own_kv_ref[1] = dv[MOST : MOST + GROUP_ROWS, :].astype(jnp.bfloat16)


def attend(lo, hi, start, end, own, left, right, grad):
    smem = pl.BlockSpec(memory_space=pltpu.SMEM)
    vmem = pl.BlockSpec(memory_space=pltpu.VMEM)
    bf16, f32 = jnp.bfloat16, jnp.float32
    return pl.pallas_call(
        attend_kernel,
        out_shape=(
            jax.ShapeDtypeStruct((GROUP, 2 * ROWS, LANES), bf16),
            jax.ShapeDtypeStruct((2, GROUP_ROWS, LANES), bf16),
            jax.ShapeDtypeStruct((2, MOST, LANES), bf16),
            jax.ShapeDtypeStruct((2, MOST, LANES), bf16),
        ),
        in_specs=[smem, smem] + [vmem] * 6,
        out_specs=(vmem,) * 4,
        scratch_shapes=[
            pltpu.VMEM((PAD_ROWS, LANES), bf16),
            pltpu.VMEM((PAD_ROWS, LANES), bf16),
            pltpu.VMEM((LANES, PAD_ROWS), bf16),
            pltpu.VMEM((LANES, PAD_ROWS), bf16),
            pltpu.VMEM((PAD_ROWS, LANES), f32),
            pltpu.VMEM((PAD_ROWS, LANES), f32),
            pltpu.VMEM((PAIR, MAX_STEPS * K_STEP, 2 * LANES), f32),
            pltpu.VMEM((PAIR, MAX_STEPS * K_STEP, 2 * LANES), f32),
            pltpu.VMEM((PAIR, LANES, LANES), f32),
            pltpu.VMEM((PAIR, LANES, LANES), f32),
        ],
        compiler_params=pltpu.CompilerParams(vmem_limit_bytes=48 * 1024 * 1024),
        cost_estimate=pl.CostEstimate(
            flops=20_000_000_000, bytes_accessed=12_000_000, transcendentals=6_000_000
        ),
        name="attend",
    )(lo, hi, start, end, own, left, right, grad)


def pack_first_kernel(k_ref, v_ref, q_ref, id_ref, out_ref):
    tags = (id_ref[...] + 1).astype(jnp.float32)
    tags = jnp.concatenate([tags, jnp.zeros((TAG_ROWS - tags.shape[0], LANES), jnp.float32)], 0)
    tags = tags.astype(jnp.bfloat16)
    for j in range(GROUP):
        cols = slice(j * LANES, (j + 1) * LANES)
        out_ref[j, 0:ROWS, :] = k_ref[:, cols]
        out_ref[j, ROWS : 2 * ROWS, :] = v_ref[:, cols]
        out_ref[j, 2 * ROWS : Q_AT, :] = tags
        out_ref[j, Q_AT : Q_AT + ROWS, :] = q_ref[:, cols]


def pack_grad_kernel(g_ref, out_ref):
    for j in range(GROUP):
        out_ref[j] = g_ref[:, j * LANES : (j + 1) * LANES]


def pack(kernel, rows, *sources):
    return pl.pallas_call(
        kernel,
        out_shape=jax.ShapeDtypeStruct((GROUP, rows, LANES), jnp.bfloat16),
        cost_estimate=pl.CostEstimate(flops=0, bytes_accessed=rows * 4096, transcendentals=0),
        name="pack",
    )(*sources)


def unpack_kernel(in_ref, x_ref, y_ref):
    for j in range(GROUP):
        cols = slice(j * LANES, (j + 1) * LANES)
        x_ref[:, cols] = in_ref[j, 0:ROWS, :]
        y_ref[:, cols] = in_ref[j, ROWS : 2 * ROWS, :]


def unpack(x):
    flat = jax.ShapeDtypeStruct((ROWS, D), jnp.bfloat16)
    return pl.pallas_call(
        unpack_kernel,
        out_shape=(flat, flat),
        cost_estimate=pl.CostEstimate(flops=0, bytes_accessed=3_200_000, transcendentals=0),
        name="unpack",
    )(x)


def total_kernel(own_ref, prev_ref, next_ref, out_ref):
    for n in range(2):
        for j in range(GROUP):
            x = own_ref[n, j * ROWS : (j + 1) * ROWS, :].astype(jnp.float32)
            if j < REACH:
                x = x + prev_ref[n, j * ROWS : (j + 1) * ROWS, :].astype(jnp.float32)
            if j >= GROUP - REACH:
                at = (j - GROUP + REACH) * ROWS
                x = x + next_ref[n, at : at + ROWS, :].astype(jnp.float32)
            out_ref[j, n * ROWS : (n + 1) * ROWS, :] = x.astype(jnp.bfloat16)


def total(own, from_prev, from_next):
    return pl.pallas_call(
        total_kernel,
        out_shape=jax.ShapeDtypeStruct((GROUP, 2 * ROWS, LANES), jnp.bfloat16),
        cost_estimate=pl.CostEstimate(flops=0, bytes_accessed=6_000_000, transcendentals=0),
        name="total",
    )(own, from_prev, from_next)


def exchange(x):
    return lax.all_to_all(x, "img", 0, 0, axis_index_groups=group_lists())


def bounds(own, left, right):
    def tags_of(x):
        return x[:, 2 * ROWS : 2 * ROWS + ROWS // LANES, :].astype(jnp.int32).reshape(-1)

    own_tags = tags_of(own)
    is_last = lax.axis_index("img") >= N_IMG - GROUP
    right_tags = jnp.where(is_last, N_IMG + 1, tags_of(right))
    ext_tags = jnp.concatenate([tags_of(left), own_tags, right_tags])
    every = jnp.arange(N_IMG + 1, dtype=jnp.int32)
    below = jnp.sum((ext_tags[None, :] < every[:, None]).astype(jnp.int32), 1)
    upto = jnp.sum((ext_tags[None, :] <= every[:, None]).astype(jnp.int32), 1)
    pick = own_tags[:, None] == every[None, :]
    start = jnp.sum(jnp.where(pick, below[None, :], 0), 1).reshape(TILES, LANES)
    end = jnp.sum(jnp.where(pick, upto[None, :], 0), 1).reshape(TILES, LANES)
    return start[:, 0], end[:, LANES - 1], start, end


def shards(queries, keys, values, out_grad, image_ids):
    ids = image_ids.reshape(ROWS // LANES, LANES)
    own = exchange(pack(pack_first_kernel, Q_AT + ROWS, keys, values, queries, ids))
    own, grad = lax.optimization_barrier((own, pack(pack_grad_kernel, ROWS, out_grad)))
    left = shifted(own[GROUP - REACH :, :Q_AT], GROUP)
    right = shifted(own[:REACH, :Q_AT], -GROUP)
    grad = exchange(grad)
    table = bounds(own, left, right)
    oq, own_kv, left_kv, right_kv = attend(*table, own, left, right, grad)
    oq = exchange(oq)
    from_next = shifted(left_kv, -GROUP)
    from_prev = shifted(right_kv, GROUP)
    attended, query_grad = unpack(oq)
    kv = exchange(total(own_kv, from_prev, from_next))
    key_grad, value_grad = unpack(kv)
    return attended, query_grad, key_grad, value_grad


def solution(mesh):
    in_specs = (P("img", None), P("img", None), P("img", None), P("img", None), P("img"))
    out_specs = (P("img", None), P("img", None), P("img", None), P("img", None))
    return jax.shard_map(shards, mesh=mesh, in_specs=in_specs, out_specs=out_specs, check_vma=False)
```

```python
import math

import jax
import jax.numpy as jnp
from jax import lax
from jax.experimental import pallas as pl
from jax.experimental.pallas import tpu as pltpu
from jax.sharding import PartitionSpec as P

D = 1024
HEAD_DIM = 64
ROWS = 384
MOST = 1152
N_IMG = 128
GROUP = 8
GROUPS = N_IMG // GROUP
GROUP_ROWS = GROUP * ROWS
REACH = 3
LANES = 128
EXT_ROWS = GROUP_ROWS + 2 * MOST
K_STEP = 256
PAD_ROWS = EXT_ROWS + K_STEP
TILES = GROUP_ROWS // LANES
TAG_ROWS = 16
Q_AT = 2 * ROWS + TAG_ROWS
MAX_STEPS = 12
UNROLLED = 8
PAIR = 2
SCALE = 1.0 / math.sqrt(HEAD_DIM)
EXP_SCALE = SCALE * math.log2(math.e)
NEG = -1e30


def group_lists():
    return [[g * GROUP + i for i in range(GROUP)] for g in range(GROUPS)]


def shifted(value, steps):
    leading, last = max(0, -steps), min(N_IMG, N_IMG - steps)
    return lax.ppermute(value, "img", [(s, s + steps) for s in range(leading, last)])


def dot_nt(a, b):
    return lax.dot_general(a, b, (((1,), (1,)), ((), ())), preferred_element_type=jnp.float32)


def dot_nn(a, b):
    return lax.dot_general(a, b, (((1,), (0,)), ((), ())), preferred_element_type=jnp.float32)


def fold_rows(x):
    return x.reshape(x.shape[0] // 8, 8, x.shape[1])


def attend_kernel(
    lo_ref, hi_ref, start_ref, end_ref, own_ref, left_ref, right_ref, g_ref,
    oq_ref, own_kv_ref, left_kv_ref, right_kv_ref,
    kx, vx, kt, vt, dk, dv, sbuf, dbuf, ot, qt,
):
    for j in range(REACH):
        a = j * ROWS
        b = MOST + GROUP_ROWS + j * ROWS
        kx[a : a + ROWS, :] = left_ref[j, 0:ROWS, :]
        vx[a : a + ROWS, :] = left_ref[j, ROWS : 2 * ROWS, :]
        kx[b : b + ROWS, :] = right_ref[j, 0:ROWS, :]
        vx[b : b + ROWS, :] = right_ref[j, ROWS : 2 * ROWS, :]
    for j in range(GROUP):
        a = MOST + j * ROWS
        kx[a : a + ROWS, :] = own_ref[j, 0:ROWS, :]
        vx[a : a + ROWS, :] = own_ref[j, ROWS : 2 * ROWS, :]
    kx[EXT_ROWS:PAD_ROWS, :] = jnp.zeros((PAD_ROWS - EXT_ROWS, LANES), jnp.bfloat16)
    vx[EXT_ROWS:PAD_ROWS, :] = jnp.zeros((PAD_ROWS - EXT_ROWS, LANES), jnp.bfloat16)
    dk[...] = jnp.zeros_like(dk)
    dv[...] = jnp.zeros_like(dv)

    def transpose_chunk(c, _):
        at = pl.multiple_of(c * K_STEP, K_STEP)
        kt[:, pl.ds(at, K_STEP)] = kx[pl.ds(at, K_STEP), :].T
        vt[:, pl.ds(at, K_STEP)] = vx[pl.ds(at, K_STEP), :].T
        return 0

    first_chunk = lo_ref[0] // K_STEP
    last_chunk = jnp.minimum(hi_ref[TILES - 1] // K_STEP + 2, PAD_ROWS // K_STEP)
    kt[...] = jnp.zeros_like(kt)
    vt[...] = jnp.zeros_like(vt)
    lax.fori_loop(first_chunk, last_chunk, transpose_chunk, 0)

    lane = lax.broadcasted_iota(jnp.int32, (LANES, LANES), 1)
    first_head = lane < HEAD_DIM
    row_index = lax.broadcasted_iota(jnp.int32, (K_STEP, LANES), 0)

    def both_heads(x):
        zero = jnp.zeros_like(x)
        return jnp.concatenate([jnp.where(first_head, x, zero), jnp.where(first_head, zero, x)], 0)

    def step_count(t):
        return (hi_ref[t] - (lo_ref[t] // LANES) * LANES + K_STEP - 1) // K_STEP

    def q_tiles(u, _):
        tiles = [u * PAIR + j for j in range(PAIR)]
        steps = step_count(tiles[0])
        for t in tiles[1:]:
            steps = jnp.maximum(steps, step_count(t))

        def sub_of(j, t, reach):
            dev = t // REACH
            off = pl.multiple_of((t % REACH) * LANES, LANES)
            k0 = jnp.minimum((lo_ref[t] // LANES) * LANES, PAD_ROWS - reach * K_STEP)
            return j, t, dev, off, k0

        def tile_part(sub, run):
            j, t, dev, off, k0 = sub
            q2 = both_heads(own_ref[dev, pl.ds(pl.multiple_of(off + Q_AT, TAG_ROWS), LANES), :])
            g2 = both_heads(g_ref[dev, pl.ds(off, LANES), :])
            begin = start_ref[pl.ds(t, 1), :]
            stop = end_ref[pl.ds(t, 1), :]

            def rows_at(i):
                return pl.ds(pl.multiple_of(k0 + i * K_STEP, LANES), K_STEP)

            def here_at(i):
                return pl.ds(i * K_STEP if isinstance(i, int) else pl.multiple_of(i * K_STEP, K_STEP), K_STEP)

            def scores(i, top):
                s = dot_nt(kx[rows_at(i), :], q2)
                index = row_index + (k0 + i * K_STEP)
                keep = (index >= begin) & (index < stop)
                s = jnp.where(jnp.concatenate([keep, keep], 1), s, NEG)
                sbuf[j, here_at(i), :] = s
                dbuf[j, here_at(i), :] = dot_nt(vx[rows_at(i), :], g2)
                return jnp.maximum(top, jnp.max(fold_rows(s), axis=0))

            def weigh(i, carry):
                top, total, delta = carry
                e = jnp.exp2((sbuf[j, here_at(i), :] - top) * EXP_SCALE)
                sbuf[j, here_at(i), :] = e
                total = total + jnp.sum(fold_rows(e), axis=0)
                delta = delta + jnp.sum(fold_rows(e * dbuf[j, here_at(i), :]), axis=0)
                return top, total, delta

            def spread(i, carry):
                inverse, delta = carry
                rows = rows_at(i)
                p = sbuf[j, here_at(i), :] * inverse
                ds = (p * (dbuf[j, here_at(i), :] - delta)).astype(jnp.bfloat16)
                p = p.astype(jnp.bfloat16)
                dv[rows, :] += dot_nn(p, g2)
                dk[rows, :] += dot_nn(ds, q2)
                o = dot_nn(vt[:, rows], p)
                dq = dot_nn(kt[:, rows], ds)
                parts = ((o, ot), (dq, qt))
                for value, ref in parts:
                    top_part = value[0:HEAD_DIM, 0:LANES]
                    low_part = value[HEAD_DIM:LANES, LANES : 2 * LANES]
                    if isinstance(i, int) and i == 0:
                        ref[j, 0:HEAD_DIM, :] = top_part
                        ref[j, HEAD_DIM:LANES, :] = low_part
                    else:
                        ref[j, 0:HEAD_DIM, :] += top_part
                        ref[j, HEAD_DIM:LANES, :] += low_part
                return carry

            def first():
                top = run(scores, jnp.full((8, 2 * LANES), NEG, jnp.float32))
                return jnp.max(top, axis=0, keepdims=True)

            def second(top):
                zeros8 = jnp.zeros((8, 2 * LANES), jnp.float32)
                _, total, delta = run(weigh, (top, zeros8, zeros8))
                inverse = 1.0 / jnp.sum(total, axis=0, keepdims=True)
                return inverse, jnp.sum(delta, axis=0, keepdims=True) * inverse

            def third(carry):
                run(spread, carry)
                oq_ref[dev, pl.ds(off, LANES), :] = ot[j].T.astype(jnp.bfloat16)
                oq_ref[dev, pl.ds(off + ROWS, LANES), :] = (qt[j].T * SCALE).astype(jnp.bfloat16)

            return first, second, third

        def whole(run):
            parts = [tile_part(sub_of(j, t, steps), run) for j, t in enumerate(tiles)]
            tops = [p[0]() for p in parts]
            stats = [p[1](top) for p, top in zip(parts, tops)]
            for p, stat in zip(parts, stats):
                p[2](stat)

        def unrolled(count):
            def run(body, carry):
                for i in range(count):
                    carry = body(i, carry)
                return carry

            return lambda: whole(run)

        def looped():
            ot[...] = jnp.zeros_like(ot)
            qt[...] = jnp.zeros_like(qt)
            for j, t in enumerate(tiles):
                turns = (step_count(t) + 1) // 2

                def run(body, carry, turns=turns):
                    two = lambda i, c: body(2 * i + 1, body(2 * i, c))
                    return lax.fori_loop(0, turns, two, carry)

                first, second, third = tile_part(sub_of(j, t, 2 * turns), run)
                third(second(first()))

        lax.switch(
            jnp.minimum(steps - 1, UNROLLED), [unrolled(c + 1) for c in range(UNROLLED)] + [looped]
        )
        return 0

    lax.fori_loop(0, TILES // PAIR, q_tiles, 0)
    left_kv_ref[0] = (dk[0:MOST, :] * SCALE).astype(jnp.bfloat16)
    left_kv_ref[1] = dv[0:MOST, :].astype(jnp.bfloat16)
    right_kv_ref[0] = (dk[MOST + GROUP_ROWS : EXT_ROWS, :] * SCALE).astype(jnp.bfloat16)
    right_kv_ref[1] = dv[MOST + GROUP_ROWS : EXT_ROWS, :].astype(jnp.bfloat16)
    own_kv_ref[0] = (dk[MOST : MOST + GROUP_ROWS, :] * SCALE).astype(jnp.bfloat16)
    own_kv_ref[1] = dv[MOST : MOST + GROUP_ROWS, :].astype(jnp.bfloat16)


def attend(lo, hi, start, end, own, left, right, grad):
    smem = pl.BlockSpec(memory_space=pltpu.SMEM)
    vmem = pl.BlockSpec(memory_space=pltpu.VMEM)
    bf16, f32 = jnp.bfloat16, jnp.float32
    return pl.pallas_call(
        attend_kernel,
        out_shape=(
            jax.ShapeDtypeStruct((GROUP, 2 * ROWS, LANES), bf16),
            jax.ShapeDtypeStruct((2, GROUP_ROWS, LANES), bf16),
            jax.ShapeDtypeStruct((2, MOST, LANES), bf16),
            jax.ShapeDtypeStruct((2, MOST, LANES), bf16),
        ),
        in_specs=[smem, smem] + [vmem] * 6,
        out_specs=(vmem,) * 4,
        scratch_shapes=[
            pltpu.VMEM((PAD_ROWS, LANES), bf16),
            pltpu.VMEM((PAD_ROWS, LANES), bf16),
            pltpu.VMEM((LANES, PAD_ROWS), bf16),
            pltpu.VMEM((LANES, PAD_ROWS), bf16),
            pltpu.VMEM((PAD_ROWS, LANES), f32),
            pltpu.VMEM((PAD_ROWS, LANES), f32),
            pltpu.VMEM((PAIR, MAX_STEPS * K_STEP, 2 * LANES), f32),
            pltpu.VMEM((PAIR, MAX_STEPS * K_STEP, 2 * LANES), f32),
            pltpu.VMEM((PAIR, LANES, LANES), f32),
            pltpu.VMEM((PAIR, LANES, LANES), f32),
        ],
        compiler_params=pltpu.CompilerParams(vmem_limit_bytes=48 * 1024 * 1024),
        cost_estimate=pl.CostEstimate(
            flops=20_000_000_000, bytes_accessed=12_000_000, transcendentals=6_000_000
        ),
        name="attend",
    )(lo, hi, start, end, own, left, right, grad)


def pack_first_kernel(k_ref, v_ref, q_ref, id_ref, out_ref):
    tags = (id_ref[...] + 1).astype(jnp.float32)
    tags = jnp.concatenate([tags, jnp.zeros((TAG_ROWS - tags.shape[0], LANES), jnp.float32)], 0)
    tags = tags.astype(jnp.bfloat16)
    for j in range(GROUP):
        cols = slice(j * LANES, (j + 1) * LANES)
        out_ref[j, 0:ROWS, :] = k_ref[:, cols]
        out_ref[j, ROWS : 2 * ROWS, :] = v_ref[:, cols]
        out_ref[j, 2 * ROWS : Q_AT, :] = tags
        out_ref[j, Q_AT : Q_AT + ROWS, :] = q_ref[:, cols]


def pack_grad_kernel(g_ref, out_ref):
    for j in range(GROUP):
        out_ref[j] = g_ref[:, j * LANES : (j + 1) * LANES]


def pack(kernel, rows, *sources):
    return pl.pallas_call(
        kernel,
        out_shape=jax.ShapeDtypeStruct((GROUP, rows, LANES), jnp.bfloat16),
        cost_estimate=pl.CostEstimate(flops=0, bytes_accessed=rows * 4096, transcendentals=0),
        name="pack",
    )(*sources)


def unpack_kernel(in_ref, x_ref, y_ref):
    for j in range(GROUP):
        cols = slice(j * LANES, (j + 1) * LANES)
        x_ref[:, cols] = in_ref[j, 0:ROWS, :]
        y_ref[:, cols] = in_ref[j, ROWS : 2 * ROWS, :]


def unpack(x):
    flat = jax.ShapeDtypeStruct((ROWS, D), jnp.bfloat16)
    return pl.pallas_call(
        unpack_kernel,
        out_shape=(flat, flat),
        cost_estimate=pl.CostEstimate(flops=0, bytes_accessed=3_200_000, transcendentals=0),
        name="unpack",
    )(x)


def total_kernel(own_ref, prev_ref, next_ref, out_ref):
    for n in range(2):
        for j in range(GROUP):
            x = own_ref[n, j * ROWS : (j + 1) * ROWS, :].astype(jnp.float32)
            if j < REACH:
                x = x + prev_ref[n, j * ROWS : (j + 1) * ROWS, :].astype(jnp.float32)
            if j >= GROUP - REACH:
                at = (j - GROUP + REACH) * ROWS
                x = x + next_ref[n, at : at + ROWS, :].astype(jnp.float32)
            out_ref[j, n * ROWS : (n + 1) * ROWS, :] = x.astype(jnp.bfloat16)


def total(own, from_prev, from_next):
    return pl.pallas_call(
        total_kernel,
        out_shape=jax.ShapeDtypeStruct((GROUP, 2 * ROWS, LANES), jnp.bfloat16),
        cost_estimate=pl.CostEstimate(flops=0, bytes_accessed=6_000_000, transcendentals=0),
        name="total",
    )(own, from_prev, from_next)


def exchange(x):
    return lax.all_to_all(x, "img", 0, 0, axis_index_groups=group_lists())


def bounds(own, left, right):
    def tags_of(x):
        return x[:, 2 * ROWS : 2 * ROWS + ROWS // LANES, :].astype(jnp.int32).reshape(-1)

    own_tags = tags_of(own)
    is_last = lax.axis_index("img") >= N_IMG - GROUP
    right_tags = jnp.where(is_last, N_IMG + 1, tags_of(right))
    ext_tags = jnp.concatenate([tags_of(left), own_tags, right_tags])
    every = jnp.arange(N_IMG + 1, dtype=jnp.int32)
    below = jnp.sum((ext_tags[None, :] < every[:, None]).astype(jnp.int32), 1)
    upto = jnp.sum((ext_tags[None, :] <= every[:, None]).astype(jnp.int32), 1)
    pick = own_tags[:, None] == every[None, :]
    start = jnp.sum(jnp.where(pick, below[None, :], 0), 1).reshape(TILES, LANES)
    end = jnp.sum(jnp.where(pick, upto[None, :], 0), 1).reshape(TILES, LANES)
    return start[:, 0], end[:, LANES - 1], start, end


def shards(queries, keys, values, out_grad, image_ids):
    ids = image_ids.reshape(ROWS // LANES, LANES)
    own = exchange(pack(pack_first_kernel, Q_AT + ROWS, keys, values, queries, ids))
    own, grad = lax.optimization_barrier((own, pack(pack_grad_kernel, ROWS, out_grad)))
    left = shifted(own[GROUP - REACH :, :Q_AT], GROUP)
    right = shifted(own[:REACH, :Q_AT], -GROUP)
    grad = exchange(grad)
    table = bounds(own, left, right)
    oq, own_kv, left_kv, right_kv = attend(*table, own, left, right, grad)
    oq = exchange(oq)
    from_next = shifted(left_kv, -GROUP)
    from_prev = shifted(right_kv, GROUP)
    attended, query_grad = unpack(oq)
    kv = exchange(total(own_kv, from_prev, from_next))
    key_grad, value_grad = unpack(kv)
    return attended, query_grad, key_grad, value_grad


def solution(mesh):
    in_specs = (P("img", None), P("img", None), P("img", None), P("img", None), P("img"))
    out_specs = (P("img", None), P("img", None), P("img", None), P("img", None))
    return jax.shard_map(shards, mesh=mesh, in_specs=in_specs, out_specs=out_specs, check_vma=False)
```

```python
import math

import jax
import jax.numpy as jnp
from jax import lax
from jax.experimental import pallas as pl
from jax.experimental.pallas import tpu as pltpu
from jax.sharding import PartitionSpec as P

D = 1024
HEAD_DIM = 64
ROWS = 384
MOST = 1152
N_IMG = 128
GROUP = 8
GROUPS = N_IMG // GROUP
GROUP_ROWS = GROUP * ROWS
REACH = 3
LANES = 128
EXT_ROWS = GROUP_ROWS + 2 * MOST
K_STEP = 256
PAD_ROWS = EXT_ROWS + K_STEP
TILES = GROUP_ROWS // LANES
TAG_ROWS = 16
Q_AT = 2 * ROWS + TAG_ROWS
MAX_STEPS = 12
UNROLLED = 8
PAIR = 2
SCALE = 1.0 / math.sqrt(HEAD_DIM)
EXP_SCALE = SCALE * math.log2(math.e)
NEG = -1e30


def group_lists():
    return [[g * GROUP + i for i in range(GROUP)] for g in range(GROUPS)]


def shifted(value, steps):
    leading, last = max(0, -steps), min(N_IMG, N_IMG - steps)
    return lax.ppermute(value, "img", [(s, s + steps) for s in range(leading, last)])


def dot_nt(a, b):
    return lax.dot_general(a, b, (((1,), (1,)), ((), ())), preferred_element_type=jnp.float32)


def dot_nn(a, b):
    return lax.dot_general(a, b, (((1,), (0,)), ((), ())), preferred_element_type=jnp.float32)


def fold_rows(x):
    return x.reshape(x.shape[0] // 8, 8, x.shape[1])


def attend_kernel(
    lo_ref, hi_ref, start_ref, end_ref, own_ref, left_ref, right_ref, g_ref,
    oq_ref, own_kv_ref, left_kv_ref, right_kv_ref,
    kx, vx, kt, vt, dk, dv, sbuf, dbuf, ot, qt,
):
    for j in range(REACH):
        a = j * ROWS
        b = MOST + GROUP_ROWS + j * ROWS
        kx[a : a + ROWS, :] = left_ref[j, 0:ROWS, :]
        vx[a : a + ROWS, :] = left_ref[j, ROWS : 2 * ROWS, :]
        kx[b : b + ROWS, :] = right_ref[j, 0:ROWS, :]
        vx[b : b + ROWS, :] = right_ref[j, ROWS : 2 * ROWS, :]
    for j in range(GROUP):
        a = MOST + j * ROWS
        kx[a : a + ROWS, :] = own_ref[j, 0:ROWS, :]
        vx[a : a + ROWS, :] = own_ref[j, ROWS : 2 * ROWS, :]
    kx[EXT_ROWS:PAD_ROWS, :] = jnp.zeros((PAD_ROWS - EXT_ROWS, LANES), jnp.bfloat16)
    vx[EXT_ROWS:PAD_ROWS, :] = jnp.zeros((PAD_ROWS - EXT_ROWS, LANES), jnp.bfloat16)
    dk[...] = jnp.zeros_like(dk)
    dv[...] = jnp.zeros_like(dv)

    def transpose_chunk(c, _):
        at = pl.multiple_of(c * K_STEP, K_STEP)
        kt[:, pl.ds(at, K_STEP)] = kx[pl.ds(at, K_STEP), :].T
        vt[:, pl.ds(at, K_STEP)] = vx[pl.ds(at, K_STEP), :].T
        return 0

    first_chunk = lo_ref[0] // K_STEP
    last_chunk = jnp.minimum(hi_ref[TILES - 1] // K_STEP + 2, PAD_ROWS // K_STEP)
    kt[...] = jnp.zeros_like(kt)
    vt[...] = jnp.zeros_like(vt)
    lax.fori_loop(first_chunk, last_chunk, transpose_chunk, 0)

    lane = lax.broadcasted_iota(jnp.int32, (LANES, LANES), 1)
    first_head = lane < HEAD_DIM
    row_index = lax.broadcasted_iota(jnp.int32, (K_STEP, LANES), 0)

    def both_heads(x):
        zero = jnp.zeros_like(x)
        return jnp.concatenate([jnp.where(first_head, x, zero), jnp.where(first_head, zero, x)], 0)

    def step_count(t):
        return (hi_ref[t] - (lo_ref[t] // LANES) * LANES + K_STEP - 1) // K_STEP

    def q_tiles(u, _):
        tiles = [u * PAIR + j for j in range(PAIR)]
        steps = step_count(tiles[0])
        for t in tiles[1:]:
            steps = jnp.maximum(steps, step_count(t))

        def sub_of(j, t, reach):
            dev = t // REACH
            off = pl.multiple_of((t % REACH) * LANES, LANES)
            k0 = jnp.minimum((lo_ref[t] // LANES) * LANES, PAD_ROWS - reach * K_STEP)
            return j, t, dev, off, k0

        def tile_part(sub, run):
            j, t, dev, off, k0 = sub
            q2 = both_heads(own_ref[dev, pl.ds(pl.multiple_of(off + Q_AT, TAG_ROWS), LANES), :])
            g2 = both_heads(g_ref[dev, pl.ds(off, LANES), :])
            begin = start_ref[pl.ds(t, 1), :]
            stop = end_ref[pl.ds(t, 1), :]

            def rows_at(i):
                return pl.ds(pl.multiple_of(k0 + i * K_STEP, LANES), K_STEP)

            def here_at(i):
                return pl.ds(i * K_STEP if isinstance(i, int) else pl.multiple_of(i * K_STEP, K_STEP), K_STEP)

            def scores(i, top):
                s = dot_nt(kx[rows_at(i), :], q2)
                index = row_index + (k0 + i * K_STEP)
                keep = (index >= begin) & (index < stop)
                s = jnp.where(jnp.concatenate([keep, keep], 1), s, NEG)
                sbuf[j, here_at(i), :] = s
                dbuf[j, here_at(i), :] = dot_nt(vx[rows_at(i), :], g2)
                return jnp.maximum(top, jnp.max(fold_rows(s), axis=0))

            def weigh(i, carry):
                top, total, delta = carry
                e = jnp.exp2((sbuf[j, here_at(i), :] - top) * EXP_SCALE)
                sbuf[j, here_at(i), :] = e
                total = total + jnp.sum(fold_rows(e), axis=0)
                delta = delta + jnp.sum(fold_rows(e * dbuf[j, here_at(i), :]), axis=0)
                return top, total, delta

            def spread(i, carry):
                inverse, delta = carry
                rows = rows_at(i)
                p = sbuf[j, here_at(i), :] * inverse
                ds = (p * (dbuf[j, here_at(i), :] - delta)).astype(jnp.bfloat16)
                p = p.astype(jnp.bfloat16)
                dv[rows, :] += dot_nn(p, g2)
                dk[rows, :] += dot_nn(ds, q2)
                o = dot_nn(vt[:, rows], p)
                dq = dot_nn(kt[:, rows], ds)
                parts = ((o, ot), (dq, qt))
                for value, ref in parts:
                    top_part = value[0:HEAD_DIM, 0:LANES]
                    low_part = value[HEAD_DIM:LANES, LANES : 2 * LANES]
                    if isinstance(i, int) and i == 0:
                        ref[j, 0:HEAD_DIM, :] = top_part
                        ref[j, HEAD_DIM:LANES, :] = low_part
                    else:
                        ref[j, 0:HEAD_DIM, :] += top_part
                        ref[j, HEAD_DIM:LANES, :] += low_part
                return carry

            def first():
                top = run(scores, jnp.full((8, 2 * LANES), NEG, jnp.float32))
                return jnp.max(top, axis=0, keepdims=True)

            def second(top):
                zeros8 = jnp.zeros((8, 2 * LANES), jnp.float32)
                _, total, delta = run(weigh, (top, zeros8, zeros8))
                inverse = 1.0 / jnp.sum(total, axis=0, keepdims=True)
                return inverse, jnp.sum(delta, axis=0, keepdims=True) * inverse

            def third(carry):
                run(spread, carry)
                oq_ref[dev, pl.ds(off, LANES), :] = ot[j].T.astype(jnp.bfloat16)
                oq_ref[dev, pl.ds(off + ROWS, LANES), :] = (qt[j].T * SCALE).astype(jnp.bfloat16)

            return first, second, third

        def whole(run):
            parts = [tile_part(sub_of(j, t, steps), run) for j, t in enumerate(tiles)]
            tops = [p[0]() for p in parts]
            stats = [p[1](top) for p, top in zip(parts, tops)]
            for p, stat in zip(parts, stats):
                p[2](stat)

        def unrolled(count):
            def run(body, carry):
                for i in range(count):
                    carry = body(i, carry)
                return carry

            return lambda: whole(run)

        def looped():
            ot[...] = jnp.zeros_like(ot)
            qt[...] = jnp.zeros_like(qt)
            for j, t in enumerate(tiles):
                turns = (step_count(t) + 2) // 3

                def run(body, carry, turns=turns):
                    three = lambda i, c: body(3 * i + 2, body(3 * i + 1, body(3 * i, c)))
                    return lax.fori_loop(0, turns, three, carry)

                first, second, third = tile_part(sub_of(j, t, 3 * turns), run)
                third(second(first()))

        lax.switch(
            jnp.minimum(steps - 1, UNROLLED), [unrolled(c + 1) for c in range(UNROLLED)] + [looped]
        )
        return 0

    lax.fori_loop(0, TILES // PAIR, q_tiles, 0)
    left_kv_ref[0] = (dk[0:MOST, :] * SCALE).astype(jnp.bfloat16)
    left_kv_ref[1] = dv[0:MOST, :].astype(jnp.bfloat16)
    right_kv_ref[0] = (dk[MOST + GROUP_ROWS : EXT_ROWS, :] * SCALE).astype(jnp.bfloat16)
    right_kv_ref[1] = dv[MOST + GROUP_ROWS : EXT_ROWS, :].astype(jnp.bfloat16)
    own_kv_ref[0] = (dk[MOST : MOST + GROUP_ROWS, :] * SCALE).astype(jnp.bfloat16)
    own_kv_ref[1] = dv[MOST : MOST + GROUP_ROWS, :].astype(jnp.bfloat16)


def attend(lo, hi, start, end, own, left, right, grad):
    smem = pl.BlockSpec(memory_space=pltpu.SMEM)
    vmem = pl.BlockSpec(memory_space=pltpu.VMEM)
    bf16, f32 = jnp.bfloat16, jnp.float32
    return pl.pallas_call(
        attend_kernel,
        out_shape=(
            jax.ShapeDtypeStruct((GROUP, 2 * ROWS, LANES), bf16),
            jax.ShapeDtypeStruct((2, GROUP_ROWS, LANES), bf16),
            jax.ShapeDtypeStruct((2, MOST, LANES), bf16),
            jax.ShapeDtypeStruct((2, MOST, LANES), bf16),
        ),
        in_specs=[smem, smem] + [vmem] * 6,
        out_specs=(vmem,) * 4,
        scratch_shapes=[
            pltpu.VMEM((PAD_ROWS, LANES), bf16),
            pltpu.VMEM((PAD_ROWS, LANES), bf16),
            pltpu.VMEM((LANES, PAD_ROWS), bf16),
            pltpu.VMEM((LANES, PAD_ROWS), bf16),
            pltpu.VMEM((PAD_ROWS, LANES), f32),
            pltpu.VMEM((PAD_ROWS, LANES), f32),
            pltpu.VMEM((PAIR, MAX_STEPS * K_STEP, 2 * LANES), f32),
            pltpu.VMEM((PAIR, MAX_STEPS * K_STEP, 2 * LANES), f32),
            pltpu.VMEM((PAIR, LANES, LANES), f32),
            pltpu.VMEM((PAIR, LANES, LANES), f32),
        ],
        compiler_params=pltpu.CompilerParams(vmem_limit_bytes=48 * 1024 * 1024),
        cost_estimate=pl.CostEstimate(
            flops=20_000_000_000, bytes_accessed=12_000_000, transcendentals=6_000_000
        ),
        name="attend",
    )(lo, hi, start, end, own, left, right, grad)


def pack_first_kernel(k_ref, v_ref, q_ref, id_ref, out_ref):
    tags = (id_ref[...] + 1).astype(jnp.float32)
    tags = jnp.concatenate([tags, jnp.zeros((TAG_ROWS - tags.shape[0], LANES), jnp.float32)], 0)
    tags = tags.astype(jnp.bfloat16)
    for j in range(GROUP):
        cols = slice(j * LANES, (j + 1) * LANES)
        out_ref[j, 0:ROWS, :] = k_ref[:, cols]
        out_ref[j, ROWS : 2 * ROWS, :] = v_ref[:, cols]
        out_ref[j, 2 * ROWS : Q_AT, :] = tags
        out_ref[j, Q_AT : Q_AT + ROWS, :] = q_ref[:, cols]


def pack_grad_kernel(g_ref, out_ref):
    for j in range(GROUP):
        out_ref[j] = g_ref[:, j * LANES : (j + 1) * LANES]


def pack(kernel, rows, *sources):
    return pl.pallas_call(
        kernel,
        out_shape=jax.ShapeDtypeStruct((GROUP, rows, LANES), jnp.bfloat16),
        cost_estimate=pl.CostEstimate(flops=0, bytes_accessed=rows * 4096, transcendentals=0),
        name="pack",
    )(*sources)


def unpack_kernel(in_ref, x_ref, y_ref):
    for j in range(GROUP):
        cols = slice(j * LANES, (j + 1) * LANES)
        x_ref[:, cols] = in_ref[j, 0:ROWS, :]
        y_ref[:, cols] = in_ref[j, ROWS : 2 * ROWS, :]


def unpack(x):
    flat = jax.ShapeDtypeStruct((ROWS, D), jnp.bfloat16)
    return pl.pallas_call(
        unpack_kernel,
        out_shape=(flat, flat),
        cost_estimate=pl.CostEstimate(flops=0, bytes_accessed=3_200_000, transcendentals=0),
        name="unpack",
    )(x)


def total_kernel(own_ref, prev_ref, next_ref, out_ref):
    for n in range(2):
        for j in range(GROUP):
            x = own_ref[n, j * ROWS : (j + 1) * ROWS, :].astype(jnp.float32)
            if j < REACH:
                x = x + prev_ref[n, j * ROWS : (j + 1) * ROWS, :].astype(jnp.float32)
            if j >= GROUP - REACH:
                at = (j - GROUP + REACH) * ROWS
                x = x + next_ref[n, at : at + ROWS, :].astype(jnp.float32)
            out_ref[j, n * ROWS : (n + 1) * ROWS, :] = x.astype(jnp.bfloat16)


def total(own, from_prev, from_next):
    return pl.pallas_call(
        total_kernel,
        out_shape=jax.ShapeDtypeStruct((GROUP, 2 * ROWS, LANES), jnp.bfloat16),
        cost_estimate=pl.CostEstimate(flops=0, bytes_accessed=6_000_000, transcendentals=0),
        name="total",
    )(own, from_prev, from_next)


def exchange(x):
    return lax.all_to_all(x, "img", 0, 0, axis_index_groups=group_lists())


def bounds(own, left, right):
    def tags_of(x):
        return x[:, 2 * ROWS : 2 * ROWS + ROWS // LANES, :].astype(jnp.int32).reshape(-1)

    own_tags = tags_of(own)
    is_last = lax.axis_index("img") >= N_IMG - GROUP
    right_tags = jnp.where(is_last, N_IMG + 1, tags_of(right))
    ext_tags = jnp.concatenate([tags_of(left), own_tags, right_tags])
    every = jnp.arange(N_IMG + 1, dtype=jnp.int32)
    below = jnp.sum((ext_tags[None, :] < every[:, None]).astype(jnp.int32), 1)
    upto = jnp.sum((ext_tags[None, :] <= every[:, None]).astype(jnp.int32), 1)
    pick = own_tags[:, None] == every[None, :]
    start = jnp.sum(jnp.where(pick, below[None, :], 0), 1).reshape(TILES, LANES)
    end = jnp.sum(jnp.where(pick, upto[None, :], 0), 1).reshape(TILES, LANES)
    return start[:, 0], end[:, LANES - 1], start, end


def shards(queries, keys, values, out_grad, image_ids):
    ids = image_ids.reshape(ROWS // LANES, LANES)
    own = exchange(pack(pack_first_kernel, Q_AT + ROWS, keys, values, queries, ids))
    own, grad = lax.optimization_barrier((own, pack(pack_grad_kernel, ROWS, out_grad)))
    left = shifted(own[GROUP - REACH :, :Q_AT], GROUP)
    right = shifted(own[:REACH, :Q_AT], -GROUP)
    grad = exchange(grad)
    table = bounds(own, left, right)
    oq, own_kv, left_kv, right_kv = attend(*table, own, left, right, grad)
    oq = exchange(oq)
    from_next = shifted(left_kv, -GROUP)
    from_prev = shifted(right_kv, GROUP)
    attended, query_grad = unpack(oq)
    kv = exchange(total(own_kv, from_prev, from_next))
    key_grad, value_grad = unpack(kv)
    return attended, query_grad, key_grad, value_grad


def solution(mesh):
    in_specs = (P("img", None), P("img", None), P("img", None), P("img", None), P("img"))
    out_specs = (P("img", None), P("img", None), P("img", None), P("img", None))
    return jax.shard_map(shards, mesh=mesh, in_specs=in_specs, out_specs=out_specs, check_vma=False)
```
